32 devices in a mesh: tomo: 4 (over y, x), brick: 8 (over z, core).
Axes of the slice: x: 2, y: 2, z: 4, core: 2. Of those that a mesh axis runs over, the one named last changes fastest.
Arguments:
- features: bfloat16 [4, 64, 512, 128], P('tomo', 'brick'), may hold values from -6 to 6
- weight: bfloat16 [27, 128, 128], replicated, may hold values from -0.109375 to 0.109375
- cotangent: bfloat16 [4, 64, 512, 128], P('tomo', 'brick'), may hold values from -6 to 6
- brick_pos: int32 [4, 64], P('tomo', 'brick'), may hold values from 0 to 7, as said below
- brick_count: int32 [4, 8], P('tomo', 'brick'), may hold values from 3 to 8, as said below
Outputs:
- output: bfloat16 [4, 64, 512, 128], P('tomo', 'brick')
- input_grad: bfloat16 [4, 64, 512, 128], P('tomo', 'brick')
- weight_grad: float32 [27, 128, 128], replicated
The draws below stay inside these ranges and needn't reach their ends.
Inputs may be any that keep to these rules, and one draw needn't show every extreme that they name: `brick_count`: in every crop some device has all 8 positions occupied. `brick_pos`: the 8 slots of one device hold each position 0 to 7 once: first the occupied positions in increasing order, then the empty ones in increasing order.
All inputs are finite; a program needn't handle non-finite values.
Results may differ from the reference program's by a relative error of at most 0.001.
Values may be sent and summed in bfloat16 or wider, within the bound.
A program may use at most 128 MiB of HBM per device.

```python
import math
import jax
import jax.numpy as jnp
from jax import lax

C = 128
BE = 8
CAP = 8
VOX = 512
SLOTS = 64
N_TOMO = 4
N_BRICK = 8


def brick_layout(key):
    key_first = jax.random.fold_in(key, 11)
    key_second = jax.random.fold_in(key, 12)
    key_full = jax.random.fold_in(key, 13)
    key_order = jax.random.fold_in(key, 14)
    factor_a = jax.random.randint(key_first, (N_TOMO, N_BRICK), 0, CAP)
    factor_b = jax.random.randint(key_second, (N_TOMO, N_BRICK), 0, CAP)
    counts = jnp.minimum(3 + (factor_a + factor_b) // 2, CAP)
    full_device = jax.random.randint(key_full, (N_TOMO, 1), 0, N_BRICK)
    counts = jnp.where(jnp.arange(N_BRICK, dtype=jnp.int32)[None, :] == full_device, CAP, counts)
    scores = jax.random.randint(key_order, (N_TOMO, N_BRICK, CAP), 0, 1 << 20) * CAP + jnp.arange(CAP, dtype=jnp.int32)
    ranking = jnp.argsort(scores, axis=-1)
    rank_of = jnp.argsort(ranking, axis=-1)
    occupied = rank_of < counts[..., None]
    slot_keys = jnp.where(occupied, 0, CAP) + jnp.arange(CAP, dtype=jnp.int32)
    positions = jnp.argsort(slot_keys, axis=-1)
    return (counts.astype(jnp.int32), positions.reshape(N_TOMO, N_BRICK * CAP).astype(jnp.int32))


def draw_brick_pos(key, part):
    counts, positions = brick_layout(key)
    return positions


def draw_brick_count(key, part):
    counts, positions = brick_layout(key)
    return counts


def block_scale(own_key, shape, shards, smallest, largest):
    gain = 1.0
    for position, shards_of in shards:
        heights = jax.random.uniform(jax.random.fold_in(jax.random.fold_in(own_key, 6), position), (shards_of,), jnp.float32, smallest / len(shards), largest / len(shards))
        gain = gain * jnp.repeat(jnp.exp(heights), shape[position] // shards_of).reshape((-1,) + (1,) * (len(shape) - 1 - position))
    return gain


def centred(rng, shape, spread, limit, pieces=(), kind=jnp.bfloat16):
    array = jax.random.normal(rng, shape, jnp.float32) * spread
    if len(pieces) > 0:
        array = block_scale(rng, shape, pieces, -0.22, 0.18) * array
    return jnp.clip(array, min=-limit, max=limit).astype(kind)


def setup_inputs(seed: int = 0) -> dict:
    key_of = jax.random.split(jax.random.key(seed), 6)
    features = centred(key_of[0], (N_TOMO, SLOTS, VOX, C), 1.0, 6.0, ((0, 4), (1, 8)))
    weight = centred(key_of[1], (27, C, C), (27 * C) ** -0.5, 0.109375)
    cotangent = centred(key_of[2], (N_TOMO, SLOTS, VOX, C), 1.0, 6.0, ((0, 4), (1, 8)))
    brick_pos = draw_brick_pos(jax.random.fold_in(key_of[5], 71), 0)
    brick_count = draw_brick_count(jax.random.fold_in(key_of[5], 71), 0)
    return dict(features=features, weight=weight, cotangent=cotangent, brick_pos=brick_pos, brick_count=brick_count)


OFFSETS = [(shift_x, shift_y, shift_z) for shift_x in (-1, 0, 1) for shift_y in (-1, 0, 1) for shift_z in (-1, 0, 1)]

def cube_coords(index, levels):
    cube_x = jnp.zeros_like(index)
    cube_y = jnp.zeros_like(index)
    cube_z = jnp.zeros_like(index)
    for level in range(levels):
        cube_x = cube_x + ((index >> 3 * level + 2 & 1) << level)
        cube_y = cube_y + ((index >> 3 * level + 1 & 1) << level)
        cube_z = cube_z + ((index >> 3 * level & 1) << level)
    return (cube_x, cube_y, cube_z)

def tap_rows(window_x, extent, shift_x, shift_y, shift_z):
    channels = window_x.shape[-1]
    window_part = lax.slice(window_x, (1 + shift_x, 1 + shift_y, 1 + shift_z, 0), (1 + shift_x + extent, 1 + shift_y + extent, 1 + shift_z + extent, channels))
    return window_part.reshape(extent * extent * extent, channels)

def reference(features, weight, cotangent, brick_pos, brick_count):
    cube_side = 1
    levels = 0
    for level in range(12):
        if cube_side * cube_side * cube_side < N_BRICK:
            cube_side = cube_side * 2
            levels = levels + 1
    bricks_side = 2 * cube_side
    grid_span = BE * bricks_side
    slot_total = N_BRICK * CAP
    slot_ids = jnp.arange(slot_total, dtype=jnp.int32)
    device = slot_ids // CAP
    local_slot = slot_ids % CAP
    cube_x, cube_y, cube_z = cube_coords(device, levels)
    brick_shape = (BE, BE, BE, C)
    window_box = (BE + 2, BE + 2, BE + 2, C)

    def dense_grid(slots, brick_x, brick_y, brick_z):
        bricks = jnp.zeros((bricks_side, bricks_side, bricks_side) + brick_shape, slots.dtype)
        bricks = bricks.at[brick_x, brick_y, brick_z].set(slots.reshape((slot_total,) + brick_shape), mode='drop')
        grid = bricks.transpose(0, 3, 1, 4, 2, 5, 6).reshape(grid_span, grid_span, grid_span, C)
        return jnp.pad(grid, ((1, 1), (1, 1), (1, 1), (0, 0)))

    def per_crop(crop_args):
        slots_x, slots_g, positions, counts = crop_args
        active = local_slot < counts[device]
        brick_x = 2 * cube_x + (positions >> 2 & 1)
        brick_y = 2 * cube_y + (positions >> 1 & 1)
        brick_z = 2 * cube_z + (positions & 1)
        dropped_x = jnp.where(active, brick_x, bricks_side)
        padded_x = dense_grid(slots_x, dropped_x, brick_y, brick_z)
        padded_g = dense_grid(slots_g, dropped_x, brick_y, brick_z)

        def per_slot(weight_acc, index):
            corner = (BE * brick_x[index], BE * brick_y[index], BE * brick_z[index], jnp.int32(0))
            window_x = lax.dynamic_slice(padded_x, corner, window_box)
            window_g = lax.dynamic_slice(padded_g, corner, window_box)
            keep = active[index]
            grad_rows = jnp.where(keep, slots_g[index], jnp.zeros_like(slots_g[index]))
            summed_y = jnp.zeros((BE * BE * BE, C), jnp.float32)
            summed_dx = jnp.zeros((BE * BE * BE, C), jnp.float32)
            kernel_terms = []
            for k, (shift_x, shift_y, shift_z) in enumerate(OFFSETS):
                rows_x = tap_rows(window_x, BE, shift_x, shift_y, shift_z)
                rows_g = tap_rows(window_g, BE, -shift_x, -shift_y, -shift_z)
                summed_y = summed_y + jnp.dot(rows_x, weight[k], preferred_element_type=jnp.float32)
                summed_dx = summed_dx + jnp.dot(rows_g, weight[k].T, preferred_element_type=jnp.float32)
                kernel_terms.append(lax.dot_general(rows_x, grad_rows, (((0,), (0,)), ((), ())), preferred_element_type=jnp.float32))
            weight_acc = weight_acc + jnp.stack(kernel_terms)
            out_y = jnp.where(keep, summed_y, jnp.zeros_like(summed_y)).astype(jnp.bfloat16)
            out_dx = jnp.where(keep, summed_dx, jnp.zeros_like(summed_dx)).astype(jnp.bfloat16)
            return (weight_acc, (out_y, out_dx))
        weight_acc, (out_y, out_dx) = lax.scan(per_slot, jnp.zeros((27, C, C), jnp.float32), slot_ids)
        return (out_y, out_dx, weight_acc)
    out_y, out_dx, accs = lax.map(per_crop, (features, cotangent, brick_pos, brick_count))
    factor = 1.0 / math.sqrt(N_TOMO * N_BRICK * CAP * BE * BE * BE)
    weight_grad = lax.optimization_barrier(jnp.sum(accs, axis=0)) * factor
    return (out_y, out_dx, weight_grad)
```

```python
import functools
import math

import jax
import jax.numpy as jnp
from jax import lax
from jax.experimental import pallas as pl
from jax.experimental.pallas import tpu as pltpu
from jax.sharding import PartitionSpec as P

BE = 8
MESH = pl.DeviceIdType.MESH


def cube_coords(index, levels):
    x = y = z = 0
    for level in range(levels):
        x += ((index >> (3 * level + 2)) & 1) << level
        y += ((index >> (3 * level + 1)) & 1) << level
        z += ((index >> (3 * level)) & 1) << level
    return x, y, z


def neighbour_pairs(devices, axis):
    levels = (devices.bit_length() - 1) // 3
    where = {cube_coords(i, levels): i for i in range(devices)}
    pairs = []
    for i in range(devices):
        c = list(cube_coords(i, levels))
        c[axis] += 1
        j = where.get(tuple(c))
        if j is not None:
            pairs.append((i, j))
    return pairs


def slot_of(pos_ref, p):
    s = jnp.int32(0)
    for k in range(8):
        s = s + jnp.where(pos_ref[k] == p, k, 0)
    return s


def build_kernel(pos_ref, cnt_ref, f_ref, g_ref, o_ref):
    p = pl.program_id(0)
    live = slot_of(pos_ref, p) < cnt_ref[0]

    @pl.when(live)
    def _():
        o_ref[0] = f_ref[0]
        o_ref[1] = g_ref[0]

    @pl.when(jnp.logical_not(live))
    def _():
        o_ref[...] = jnp.zeros_like(o_ref)


def build_cubes(features, cotangent, pos, cnt):
    slots, vox, ch = features.shape
    f = features.reshape(slots, BE, BE, BE, ch)
    g = cotangent.reshape(slots, BE, BE, BE, ch)
    e = 2 * BE
    in_spec = pl.BlockSpec(
        (1, BE, BE, BE, ch), lambda p, pos, cnt: (slot_of(pos, p), 0, 0, 0, 0)
    )
    return pl.pallas_call(
        build_kernel,
        out_shape=jax.ShapeDtypeStruct((2, e, e, e, ch), features.dtype),
        grid_spec=pltpu.PrefetchScalarGridSpec(
            num_scalar_prefetch=2,
            grid=(8,),
            in_specs=[in_spec, in_spec],
            out_specs=pl.BlockSpec(
                (2, BE, BE, BE, ch),
                lambda p, pos, cnt: (0, p // 4, p // 2 % 2, p % 2, 0),
            ),
        ),
        name="build_cubes",
    )(pos, cnt, f, g)


def exchange(low_face, high_face, devices, axis):
    up = neighbour_pairs(devices, axis)
    down = [(j, i) for i, j in up]
    below = lax.ppermute(high_face, "brick", up)
    above = lax.ppermute(low_face, "brick", down)
    return below, above


def halos(cubes, devices):
    xlo, xhi = exchange(cubes[:, 0], cubes[:, -1], devices, 0)

    def yface(k):
        return jnp.concatenate([xlo[:, None, k], cubes[:, :, k], xhi[:, None, k]], axis=1)

    ylo, yhi = exchange(yface(0), yface(-1), devices, 1)

    def zface(k):
        mid = jnp.concatenate(
            [xlo[:, None, :, k], cubes[:, :, :, k], xhi[:, None, :, k]], axis=1
        )
        return jnp.concatenate([ylo[:, :, None, k], mid, yhi[:, :, None, k]], axis=2)

    zlo, zhi = exchange(zface(0), zface(-1), devices, 2)
    return xlo, xhi, ylo, yhi, zlo, zhi


def conv_kernel(
    pos_ref, cnt_ref, cube, xlo, xhi, ylo, yhi, zlo, zhi, w_ref,
    out_ref, dx_ref, dw_ref,
    pad, wf, wb, gt, obuf,
):
    e = cube.shape[1]
    ch = cube.shape[-1]
    half = e // 2
    zidx = lax.broadcasted_iota(jnp.int32, (1, e, 1), 1)

    for a in range(2):
        pad[a, 1, pl.ds(1, e), 0, 0] = ylo[a, pl.ds(1, e)]
        pad[a, 1, 0, 0, 0] = ylo[a, 0]
        pad[a, 1, e + 1, 0, 0] = ylo[a, e + 1]
        pad[a, 1, pl.ds(0, e + 2), half, 1] = yhi[a]
        for y in range(e):
            pad[a, 1, 0, (y + 1) // 2, (y + 1) % 2] = xlo[a, y]
            pad[a, 1, e + 1, (y + 1) // 2, (y + 1) % 2] = xhi[a, y]

    def fill(x, carry):
        for a in range(2):
            for y in range(e):
                pad[a, 1, x + 1, (y + 1) // 2, (y + 1) % 2] = cube[a, x, y]
        return carry

    lax.fori_loop(0, e, fill, 0)

    def shift(x, carry):
        for a in range(2):
            mid = pad[a, 1, x].reshape(e + 2, e, ch).astype(jnp.float32)
            lo = zlo[a, x][:, None, :]
            hi = zhi[a, x][:, None, :]
            down = jnp.where(zidx == 0, lo, pltpu.roll(mid, 1, 1))
            up = jnp.where(zidx == e - 1, hi, pltpu.roll(mid, e - 1, 1))
            pad[a, 0, x] = down.astype(pad.dtype).reshape(half + 1, 2, e, ch)
            pad[a, 2, x] = up.astype(pad.dtype).reshape(half + 1, 2, e, ch)
        return carry

    lax.fori_loop(0, e + 2, shift, 0)

    def rows(a, oz, x0, nx):
        parts = [
            pad[a, oz, pl.ds(x0, nx), pl.ds(i // 2, half), i % 2].reshape(nx * half * e, ch)
            for i in range(4)
        ]
        return jnp.concatenate(parts, axis=1)

    zero = jnp.zeros((ch, ch), wf.dtype)
    for t in range(9):
        ox, oz = t // 3, t % 3
        for i in range(4):
            for p in range(2):
                oy = i - p
                at = (t, pl.ds(i * ch, ch), pl.ds(p * ch, ch))
                if 0 <= oy <= 2:
                    wf[at] = w_ref[ox * 9 + oy * 3 + oz]
                    wb[at] = w_ref[(2 - ox) * 9 + (2 - oy) * 3 + 2 - oz].T
                else:
                    wf[at] = zero
                    wb[at] = zero

    def turn(x, carry):
        own = [
            pad[1, 1, x + 1, pl.ds(0, half), 1].reshape(half * e, ch),
            pad[1, 1, x + 1, pl.ds(1, half), 0].reshape(half * e, ch),
        ]
        for p in range(2):
            gt[x // 2, pl.ds(p * ch, ch), pl.ds(pl.multiple_of(x % 2 * half * e, 128), half * e)] = own[p].T
        return carry

    lax.fori_loop(0, e, turn, 0)

    def terms(t, carry):
        ox, oz = t // 3, t % 3
        acc = jnp.zeros((2 * ch, 4 * ch), jnp.float32)
        for c in range(half):
            acc = acc + jnp.dot(
                gt[c], rows(0, oz, ox + 2 * c, 2), preferred_element_type=jnp.float32
            )
        for oy in range(3):
            block = acc[:ch, oy * ch:(oy + 1) * ch] + acc[ch:, (oy + 1) * ch:(oy + 2) * ch]
            dw_ref[ox * 9 + oy * 3 + oz] = block.T
        return carry

    lax.fori_loop(0, 9, terms, 0)

    nx = 4
    for a, wts, dst in ((0, wf, out_ref), (1, wb, dx_ref)):

        def chunk(c, carry, a=a, wts=wts):
            x0 = c * nx
            acc = jnp.zeros((nx * half * e, 2 * ch), jnp.float32)
            for t in range(9):
                acc = acc + jnp.dot(
                    rows(a, t % 3, x0 + t // 3, nx), wts[t], preferred_element_type=jnp.float32
                )
            for p in range(2):
                obuf[pl.ds(x0, nx), :, p] = (
                    acc[:, p * ch:(p + 1) * ch]
                    .reshape(nx, half, 2, BE, ch)
                    .astype(obuf.dtype)
                )
            return carry

        lax.fori_loop(0, e // nx, chunk, 0)

        def put(s, carry, dst=dst):
            p = pos_ref[s]
            live = s < cnt_ref[0]

            @pl.when(live)
            def _():
                brick = obuf[pl.ds(p // 4 * BE, BE), pl.ds(p // 2 % 2 * (BE // 2), BE // 2), :, p % 2]
                dst[s] = brick.reshape(BE, BE, BE, ch)

            @pl.when(jnp.logical_not(live))
            def _():
                dst[s] = jnp.zeros((BE, BE, BE, ch), dst.dtype)

            return carry

        lax.fori_loop(0, 8, put, 0)


def convolve(cubes, faces, weight, pos, cnt):
    e = cubes.shape[1]
    ch = cubes.shape[-1]
    half = e // 2
    vm = pl.BlockSpec(memory_space=pltpu.VMEM)
    sm = pl.BlockSpec(memory_space=pltpu.SMEM)
    brick = jax.ShapeDtypeStruct((8, BE, BE, BE, ch), jnp.bfloat16)
    xlo, xhi, ylo, yhi, zlo, zhi = faces
    flops = 3 * 2 * 27 * e**3 * ch * ch
    return pl.pallas_call(
        conv_kernel,
        out_shape=(brick, brick, jax.ShapeDtypeStruct((27, ch, ch), jnp.float32)),
        in_specs=[sm, sm] + [vm] * 8,
        out_specs=(vm, vm, vm),
        scratch_shapes=[
            pltpu.VMEM((2, 3, e + 2, half + 1, 2, e, ch), jnp.bfloat16),
            pltpu.VMEM((9, 4 * ch, 2 * ch), jnp.bfloat16),
            pltpu.VMEM((9, 4 * ch, 2 * ch), jnp.bfloat16),
            pltpu.VMEM((half, 2 * ch, 2 * half * e), jnp.bfloat16),
            pltpu.VMEM((e, half, 2, 2, BE, ch), jnp.bfloat16),
        ],
        compiler_params=pltpu.CompilerParams(vmem_limit_bytes=58 << 20),
        cost_estimate=pl.CostEstimate(flops=flops, bytes_accessed=12 << 20, transcendentals=0),
        name="convolve",
    )(pos, cnt, cubes, xlo, xhi, ylo, yhi, zlo.astype(jnp.float32), zhi.astype(jnp.float32), weight)


def steps_of(n_tomo, n_brick):
    tb = n_tomo.bit_length() - 1
    bb = n_brick.bit_length() - 1
    return tb, bb


def sum_kernel(factor, tb, bb, src, out, acc, land, send, recv, gsend, grecv):
    tomo = lax.axis_index("tomo")
    brick = lax.axis_index("brick")
    core = lax.rem(brick, 2)
    total = src.shape[0]

    def flip(v, width):
        bit = lax.rem(v // width, 2)
        return bit, v + width - 2 * width * bit

    plan = []
    bit, mate = flip(brick, 1)
    plan.append((bit, (tomo, mate)))
    for k in range(tb):
        width = jnp.where(core == 0, 1 << k, 1 << (tb - 1 - k))
        bit = lax.rem(tomo // width, 2)
        plan.append((bit, (tomo + width - 2 * width * bit, brick)))
    for k in range(1, bb):
        bit, mate = flip(brick, 1 << k)
        plan.append((bit, (tomo, mate)))

    barrier = pltpu.get_barrier_semaphore()
    for _, mate in plan:
        pl.semaphore_signal(barrier, inc=1, device_id=mate, device_id_type=MESH)
    pl.semaphore_wait(barrier, len(plan))

    off = 0
    size = total
    spot = 0
    trail = []
    for k, (bit, mate) in enumerate(plan):
        size //= 2
        keep = pl.multiple_of(off + bit * size, 8)
        give = pl.multiple_of(off + (1 - bit) * size, 8)
        held = src if k == 0 else acc
        copy = pltpu.make_async_remote_copy(
            src_ref=held.at[pl.ds(give, size)],
            dst_ref=land.at[pl.ds(spot, size)],
            send_sem=send.at[k],
            recv_sem=recv.at[k],
            device_id=mate,
            device_id_type=MESH,
        )
        copy.start()
        copy.wait()
        if k < len(plan) - 1:
            acc[pl.ds(keep, size)] = held[pl.ds(keep, size)] + land[pl.ds(spot, size)]
        else:
            out[pl.ds(keep, size)] = (held[pl.ds(keep, size)] + land[pl.ds(spot, size)]) * factor
        spot += size
        trail.append((off, keep, size, mate))
        off = keep

    for k in reversed(range(len(plan))):
        off, keep, size, mate = trail[k]
        copy = pltpu.make_async_remote_copy(
            src_ref=out.at[pl.ds(keep, size)],
            dst_ref=out.at[pl.ds(keep, size)],
            send_sem=gsend.at[k],
            recv_sem=grecv.at[k],
            device_id=mate,
            device_id_type=MESH,
        )
        copy.start()
        copy.wait()


def sum_all(terms, factor, n_tomo, n_brick):
    tb, bb = steps_of(n_tomo, n_brick)
    rows, ch = terms.shape
    n = n_tomo * n_brick
    per = -(-rows // (8 * n)) * 8
    total = per * n
    padded = jnp.pad(terms, ((0, total - rows), (0, 0)))
    vm = pl.BlockSpec(memory_space=pltpu.VMEM)
    k = tb + bb
    summed = pl.pallas_call(
        functools.partial(sum_kernel, factor, tb, bb),
        out_shape=jax.ShapeDtypeStruct((total, ch), jnp.float32),
        in_specs=[vm],
        out_specs=vm,
        scratch_shapes=[
            pltpu.VMEM((total, ch), jnp.float32),
            pltpu.VMEM((total, ch), jnp.float32),
            pltpu.SemaphoreType.DMA((k,)),
            pltpu.SemaphoreType.DMA((k,)),
            pltpu.SemaphoreType.DMA((k,)),
            pltpu.SemaphoreType.DMA((k,)),
        ],
        compiler_params=pltpu.CompilerParams(collective_id=0, has_side_effects=True),
        name="sum_all",
    )(padded)
    return summed[:rows]


def shards(features, weight, cotangent, brick_pos, brick_count):
    slots, vox, ch = features.shape[1:]
    n_tomo, n_brick = lax.axis_size("tomo"), lax.axis_size("brick")
    pos, cnt = brick_pos[0], brick_count[0]
    cubes = build_cubes(features[0], cotangent[0], pos, cnt)
    faces = halos(cubes, n_brick)
    out, dx, dw = convolve(cubes, faces, weight, pos, cnt)
    factor = 1.0 / math.sqrt(n_tomo * n_brick * slots * vox)
    dw = sum_all(dw.reshape(-1, ch), factor, n_tomo, n_brick).reshape(dw.shape)
    return out.reshape(1, slots, vox, ch), dx.reshape(1, slots, vox, ch), dw


def solution(mesh):
    in_specs = (
        P("tomo", "brick", None, None),
        P(),
        P("tomo", "brick", None, None),
        P("tomo", "brick"),
        P("tomo", "brick"),
    )
    out_specs = (P("tomo", "brick", None, None), P("tomo", "brick", None, None), P())
    return jax.shard_map(shards, mesh=mesh, in_specs=in_specs, out_specs=out_specs, check_vma=False)
```

```python
import functools
import math

import jax
import jax.numpy as jnp
from jax import lax
from jax.experimental import pallas as pl
from jax.experimental.pallas import tpu as pltpu
from jax.sharding import PartitionSpec as P

BE = 8
MESH = pl.DeviceIdType.MESH
UNIT = 8


def coords_of(index, levels):
    out = []
    for bit in (2, 1, 0):
        c = 0
        for level in range(levels):
            c = c + lax.rem(index // (1 << (3 * level + bit)), 2) * (1 << level)
        out.append(c)
    return out


def index_of(coords, levels):
    i = 0
    for bit, c in zip((2, 1, 0), coords):
        for level in range(levels):
            i = i + lax.rem(c // (1 << level), 2) * (1 << (3 * level + bit))
    return i


def kernel(
    factor, tb, bb, streams,
    pos_ref, cnt_ref, f_ref, g_ref, w_ref,
    out_ref, dx_ref, tot,
    pad, zs, zr, wx, gt, obuf, src, land,
    hsend, hrecv, rsend, rrecv, gsend, grecv,
):
    e = 2 * BE
    half = e // 2
    ch = f_ref.shape[-1]
    levels = bb // 3
    side = 1 << levels
    tomo = lax.axis_index("tomo")
    brick = lax.axis_index("brick")
    here = coords_of(brick, levels)

    near = []
    for axis in range(3):
        above, below = list(here), list(here)
        above[axis] = here[axis] + 1
        below[axis] = here[axis] + side - 1
        near.append((
            here[axis] < side - 1, (tomo, index_of(above, levels)),
            here[axis] > 0, (tomo, index_of(below, levels)),
        ))

    def mate_on(v, width):
        bit = lax.rem(v // width, 2)
        return bit, v + width - 2 * width * bit

    core = mate_on(brick, 1)
    core = (core[0], (tomo, core[1]))
    tomos = []
    for k in range(tb):
        bit, mate = mate_on(tomo, 1 << k)
        tomos.append((bit, (mate, brick)))
    rest = []
    for k in range(1, bb):
        bit, mate = mate_on(brick, 1 << k)
        rest.append((bit, (tomo, mate)))
    orders = ([core] + tomos + rest, [core] + tomos[::-1] + rest)
    stages = len(orders[0])

    barrier = pltpu.get_barrier_semaphore()
    count = stages
    for _, mate in orders[0]:
        pl.semaphore_signal(barrier, inc=1, device_id=mate, device_id_type=MESH)
    for has_above, above, has_below, below in near:
        for has, mate in ((has_above, above), (has_below, below)):

            @pl.when(has)
            def _(mate=mate):
                pl.semaphore_signal(barrier, inc=1, device_id=mate, device_id_type=MESH)

            count = count + has.astype(jnp.int32)

    slots = []
    for p in range(8):
        s = jnp.int32(0)
        for k in range(8):
            s = jnp.where(pos_ref[k] == p, k, s)
        slots.append(s)

    def gather(x, carry):
        for a, ref in ((0, f_ref), (1, g_ref)):
            for q in range(4):
                parts = []
                for pz in range(2):
                    s = slots[2 * q + pz]
                    v = ref[s, x].astype(jnp.float32)
                    parts.append(jnp.where(s < cnt_ref[0], v, 0.0))
                pad[a, 1, 1 + q // 2 * BE + x, pl.ds(1 + q % 2 * BE, BE)] = jnp.concatenate(
                    parts, axis=1
                ).astype(pad.dtype)
        return carry

    lax.fori_loop(0, BE, gather, 0)
    pl.semaphore_wait(barrier, count)

    def face(axis, at):
        if axis == 0:
            return pad.at[:, 1, at, pl.ds(1, e)]
        return pad.at[:, 1, :, at]

    def ends(axis):
        if axis == 2:
            return (zs.at[0], zr.at[0]), (zs.at[1], zr.at[1])
        return (face(axis, e), face(axis, 0)), (face(axis, 1), face(axis, e + 1))

    def halo_copies(axis):
        has_above, above, has_below, below = near[axis]
        up, down = ends(axis)
        made = []
        for k, (ends_k, mate) in enumerate(((up, above), (down, below))):
            made.append(pltpu.make_async_remote_copy(
                src_ref=ends_k[0], dst_ref=ends_k[1],
                send_sem=hsend.at[axis, k], recv_sem=hrecv.at[axis, k],
                device_id=mate, device_id_type=MESH,
            ))
        return made, (has_above, has_below)

    def halo_start(axis):
        made, has = halo_copies(axis)
        for k in range(2):

            @pl.when(has[k])
            def _(k=k):
                made[k].start()

    def halo_finish(axis):
        made, has = halo_copies(axis)
        for k in range(2):

            @pl.when(has[1 - k])
            def _(k=k):
                made[k].wait_recv()

            @pl.when(jnp.logical_not(has[1 - k]))
            def _(k=k):
                if axis == 0:
                    pad[:, 1, (0, e + 1)[k], pl.ds(1, e)] = jnp.zeros((2, e, e, ch), pad.dtype)
                elif axis == 1:
                    pad[:, 1, :, (0, e + 1)[k]] = jnp.zeros((2, e + 2, e, ch), pad.dtype)
                else:
                    zr[k] = jnp.zeros((2, e + 2, e + 2, ch), zr.dtype)

            @pl.when(has[k])
            def _(k=k):
                made[k].wait_send()

    halo_start(0)

    zero = jnp.zeros((ch, ch), wx.dtype)

    def spread(t, carry):
        ox, oz = t // 3, lax.rem(t, 3)
        for i in range(4):
            for p in range(2):
                oy = i - p
                at = (pl.ds(i * ch, ch), pl.ds(p * ch, ch))
                if 0 <= oy <= 2:
                    wx[(0, t) + at] = w_ref[ox * 9 + oy * 3 + oz]
                    wx[(1, t) + at] = w_ref[(2 - ox) * 9 + (2 - oy) * 3 + 2 - oz].T
                else:
                    wx[(0, t) + at] = zero
                    wx[(1, t) + at] = zero
        return carry

    lax.fori_loop(0, 9, spread, 0)
    halo_finish(0)
    halo_start(1)

    def turn(c, carry):
        for x in range(2):
            own = pad[1, 1, 2 * c + x + 1, pl.ds(1, e)].reshape(half, 2, e, ch)
            for p in range(2):
                gt[c, pl.ds(p * ch, ch), pl.ds(x * half * e, half * e)] = (
                    own[:, p].reshape(half * e, ch).T
                )
        return carry

    lax.fori_loop(0, half, turn, 0)
    halo_finish(1)

    def edges(x, carry):
        for a in range(2):
            v = pad[a, 1, x].astype(jnp.float32)
            zs[0, a, x] = v[:, e - 1]
            zs[1, a, x] = v[:, 0]
        return carry

    lax.fori_loop(0, e + 2, edges, 0)
    halo_start(2)
    halo_finish(2)

    zidx = lax.broadcasted_iota(jnp.int32, (1, e, 1), 1)

    def shift(a):
        def body(x, carry):
            mid = pad[a, 1, x].astype(jnp.float32)
            lo = zr[0, a, x][:, None, :]
            hi = zr[1, a, x][:, None, :]
            pad[a, 0, x] = jnp.where(zidx == 0, lo, pltpu.roll(mid, 1, 1)).astype(pad.dtype)
            pad[a, 2, x] = jnp.where(zidx == e - 1, hi, pltpu.roll(mid, e - 1, 1)).astype(pad.dtype)
            return carry

        lax.fori_loop(0, e + 2, body, 0)

    def rows(a, oz, x0, nx):
        v = pad[a, oz, pl.ds(x0, nx)].reshape(nx, half + 1, 2, e, ch)
        parts = [
            v[:, i // 2:i // 2 + half, i % 2].reshape(nx * half * e, ch) for i in range(4)
        ]
        return jnp.concatenate(parts, axis=1)

    def terms(t, carry):
        ox, oz = t // 3, lax.rem(t, 3)
        acc = jnp.zeros((2 * ch, 4 * ch), jnp.float32)
        for c in range(half):
            acc = acc + jnp.dot(
                gt[c], rows(0, oz, ox + 2 * c, 2), preferred_element_type=jnp.float32
            )
        for oy in range(3):
            block = acc[:ch, oy * ch:(oy + 1) * ch] + acc[ch:, (oy + 1) * ch:(oy + 2) * ch]
            src[pl.ds(pl.multiple_of((t * 3 + oy) * ch, ch), ch)] = block.T
        return carry

    routes = []
    spot = 0
    for base, size, order in streams:
        off = base
        route = []
        for bit, mate in orders[order]:
            size = size // 2
            route.append((
                pl.multiple_of(off + bit * size, UNIT),
                pl.multiple_of(off + size - bit * size, UNIT),
                size, spot, mate,
            ))
            off = off + bit * size
            spot += size
        routes.append(route)
    flying = {}

    def begin(s, j):
        down = j < stages
        k = j if down else 2 * stages - 1 - j
        keep, give, size, at, mate = routes[s][k]
        if down:
            copy = pltpu.make_async_remote_copy(
                src_ref=src.at[pl.ds(give, size)], dst_ref=land.at[pl.ds(at, size)],
                send_sem=rsend.at[s, k], recv_sem=rrecv.at[s, k],
                device_id=mate, device_id_type=MESH,
            )
        else:
            copy = pltpu.make_async_remote_copy(
                src_ref=tot.at[pl.ds(keep, size)], dst_ref=tot.at[pl.ds(keep, size)],
                send_sem=gsend.at[s, k], recv_sem=grecv.at[s, k],
                device_id=mate, device_id_type=MESH,
            )
        copy.start()
        flying[s] = copy

    def end(s, j):
        flying[s].wait()
        if j < stages:
            keep, give, size, at, mate = routes[s][j]
            both = src[pl.ds(keep, size)] + land[pl.ds(at, size)]
            if j < stages - 1:
                src[pl.ds(keep, size)] = both
            else:
                tot[pl.ds(keep, size)] = both * factor

    nx = 4

    def conv(a, c):
        x0 = c * nx
        acc = jnp.zeros((nx * half * e, 2 * ch), jnp.float32)
        for t in range(9):
            acc = acc + jnp.dot(
                rows(a, t % 3, x0 + t // 3, nx), wx[a, t], preferred_element_type=jnp.float32
            )
        for p in range(2):
            obuf[a, pl.ds(x0, nx), :, p] = (
                acc[:, p * ch:(p + 1) * ch].reshape(nx, half, 2, BE, ch).astype(obuf.dtype)
            )

    def put(a, dst):
        for s in range(8):
            p = pos_ref[s]
            v = obuf[
                a, pl.ds(p // 4 * BE, BE), pl.ds(lax.rem(p // 2, 2) * (BE // 2), BE // 2), :,
                lax.rem(p, 2),
            ].reshape(BE, BE, BE, ch)
            dst[s] = jnp.where(s < cnt_ref[0], v, jnp.zeros_like(v))

    work = []
    for a, dst in ((0, out_ref), (1, dx_ref)):
        if a == 1:
            work.append(functools.partial(shift, 1))
        for c in range(e // nx):
            work.append(functools.partial(conv, a, c))
        work.append(functools.partial(put, a, dst))

    lead = streams[2][0]
    early = min(9, -(-lead // (3 * ch)))
    first = (0, 1)
    second = (2, 3)
    used = 3 * 9 * ch
    shift(0)
    if src.shape[0] > used:
        src[pl.ds(used, src.shape[0] - used)] = jnp.zeros((src.shape[0] - used, ch), src.dtype)
    lax.fori_loop(0, early, terms, 0)
    for s in first:
        begin(s, 0)
    if early < 9:
        lax.fori_loop(early, 9, terms, 0)
    last = 2 * stages - 1
    skew = 1
    for tau in range(1, last + 2 + skew):
        for group, j in ((first, tau), (second, tau - skew)):
            for s in group:
                if 1 <= j <= last + 1:
                    end(s, j - 1)
                if 0 <= j <= last:
                    begin(s, j)
        for _ in range(1 if tau < last + skew else len(work)):
            if work:
                work.pop(0)()


def fused(features, cotangent, weight, pos, cnt, factor, n_tomo, n_brick):
    slots, vox, ch = features.shape
    e = 2 * BE
    half = e // 2
    n = n_tomo * n_brick
    tb, bb = n_tomo.bit_length() - 1, n_brick.bit_length() - 1
    stages = tb + bb
    rows = weight.shape[0] * ch
    unit = UNIT * n
    units = -(-rows // unit)
    units = max(units, 4)
    lead = 5 * 3 * ch // unit
    lead = min(lead, units // 2) if lead >= 2 else 2
    parts = [lead - lead // 2, lead // 2, units - lead - (units - lead) // 2, (units - lead) // 2]
    streams = []
    base = 0
    for k, u in enumerate(parts):
        streams.append((base, u * unit, k % 2))
        base += u * unit
    total = base
    vm = pl.BlockSpec(memory_space=pltpu.VMEM)
    sm = pl.BlockSpec(memory_space=pltpu.SMEM)
    brick = jax.ShapeDtypeStruct((slots, BE, BE, BE, ch), jnp.bfloat16)
    dma = pltpu.SemaphoreType.DMA
    out, dx, tot = pl.pallas_call(
        functools.partial(kernel, factor, tb, bb, streams),
        out_shape=(brick, brick, jax.ShapeDtypeStruct((total, ch), jnp.float32)),
        in_specs=[sm, sm, vm, vm, vm],
        out_specs=(vm, vm, vm),
        scratch_shapes=[
            pltpu.VMEM((2, 3, e + 2, e + 2, e, ch), jnp.bfloat16),
            pltpu.VMEM((2, 2, e + 2, e + 2, ch), jnp.float32),
            pltpu.VMEM((2, 2, e + 2, e + 2, ch), jnp.float32),
            pltpu.VMEM((2, 9, 4 * ch, 2 * ch), jnp.bfloat16),
            pltpu.VMEM((half, 2 * ch, 2 * half * e), jnp.bfloat16),
            pltpu.VMEM((2, e, half, 2, 2, BE, ch), jnp.bfloat16),
            pltpu.VMEM((total, ch), jnp.float32),
            pltpu.VMEM((total, ch), jnp.float32),
            dma((3, 2)), dma((3, 2)),
            dma((4, stages)), dma((4, stages)), dma((4, stages)), dma((4, stages)),
        ],
        compiler_params=pltpu.CompilerParams(
            collective_id=0, has_side_effects=True, vmem_limit_bytes=58 << 20
        ),
        name="fused",
    )(
        pos, cnt,
        features.reshape(slots, BE, BE, BE, ch), cotangent.reshape(slots, BE, BE, BE, ch), weight,
    )
    dw = tot[:rows].reshape(3, 3, 3, ch, ch).transpose(0, 2, 1, 3, 4).reshape(weight.shape)
    return out, dx, dw


def shards(features, weight, cotangent, brick_pos, brick_count):
    slots, vox, ch = features.shape[1:]
    n_tomo, n_brick = lax.axis_size("tomo"), lax.axis_size("brick")
    factor = 1.0 / math.sqrt(n_tomo * n_brick * slots * vox)
    out, dx, dw = fused(
        features[0], cotangent[0], weight, brick_pos[0], brick_count[0], factor, n_tomo, n_brick
    )
    return out.reshape(1, slots, vox, ch), dx.reshape(1, slots, vox, ch), dw


def solution(mesh):
    in_specs = (
        P("tomo", "brick", None, None),
        P(),
        P("tomo", "brick", None, None),
        P("tomo", "brick"),
        P("tomo", "brick"),
    )
    out_specs = (P("tomo", "brick", None, None), P("tomo", "brick", None, None), P())
    return jax.shard_map(shards, mesh=mesh, in_specs=in_specs, out_specs=out_specs, check_vma=False)
```

```python
import functools
import math

import jax
import jax.numpy as jnp
from jax import lax
from jax.experimental import pallas as pl
from jax.experimental.pallas import tpu as pltpu
from jax.sharding import PartitionSpec as P

BE = 8
MESH = pl.DeviceIdType.MESH
UNIT = 8


def coords_of(index, levels):
    out = []
    for bit in (2, 1, 0):
        c = 0
        for level in range(levels):
            c = c + lax.rem(index // (1 << (3 * level + bit)), 2) * (1 << level)
        out.append(c)
    return out


def index_of(coords, levels):
    i = 0
    for bit, c in zip((2, 1, 0), coords):
        for level in range(levels):
            i = i + lax.rem(c // (1 << level), 2) * (1 << (3 * level + bit))
    return i


def kernel(
    factor, tb, bb, streams,
    pos_ref, cnt_ref, f_ref, g_ref, w_ref,
    out_ref, dx_ref, dw_ref,
    pad, zs, zr, wx, gt, obuf, src, land, tot,
    hsend, hrecv, rsend, rrecv, gsend, grecv,
):
    e = 2 * BE
    half = e // 2
    ch = f_ref.shape[-1]
    levels = bb // 3
    side = 1 << levels
    tomo = lax.axis_index("tomo")
    brick = lax.axis_index("brick")
    here = coords_of(brick, levels)

    near = []
    for axis in range(3):
        above, below = list(here), list(here)
        above[axis] = here[axis] + 1
        below[axis] = here[axis] + side - 1
        near.append((
            here[axis] < side - 1, (tomo, index_of(above, levels)),
            here[axis] > 0, (tomo, index_of(below, levels)),
        ))

    def mate_on(v, width):
        bit = lax.rem(v // width, 2)
        return bit, v + width - 2 * width * bit

    core = mate_on(brick, 1)
    core = (core[0], (tomo, core[1]))
    tomos = []
    for k in range(tb):
        bit, mate = mate_on(tomo, 1 << k)
        tomos.append((bit, (mate, brick)))
    rest = []
    for k in range(1, bb):
        bit, mate = mate_on(brick, 1 << k)
        rest.append((bit, (tomo, mate)))
    orders = ([core] + tomos + rest, [core] + tomos[::-1] + rest)
    stages = len(orders[0])

    barrier = pltpu.get_barrier_semaphore()
    count = stages
    for _, mate in orders[0]:
        pl.semaphore_signal(barrier, inc=1, device_id=mate, device_id_type=MESH)
    for has_above, above, has_below, below in near:
        for has, mate in ((has_above, above), (has_below, below)):

            @pl.when(has)
            def _(mate=mate):
                pl.semaphore_signal(barrier, inc=1, device_id=mate, device_id_type=MESH)

            count = count + has.astype(jnp.int32)

    slots = []
    for p in range(8):
        s = jnp.int32(0)
        for k in range(8):
            s = jnp.where(pos_ref[k] == p, k, s)
        slots.append(s)

    def gather(x, carry):
        for a, ref in ((0, f_ref), (1, g_ref)):
            for q in range(4):
                parts = []
                for pz in range(2):
                    s = slots[2 * q + pz]
                    v = ref[s, x].astype(jnp.float32)
                    parts.append(jnp.where(s < cnt_ref[0], v, 0.0))
                pad[a, 1, 1 + q // 2 * BE + x, pl.ds(1 + q % 2 * BE, BE)] = jnp.concatenate(
                    parts, axis=1
                ).astype(pad.dtype)
        return carry

    lax.fori_loop(0, BE, gather, 0)
    pl.semaphore_wait(barrier, count)

    def face(axis, a, at):
        if axis == 0:
            return pad.at[a, 1, at, pl.ds(1, e)]
        return pad.at[a, 1, :, at]

    def ends(axis, a):
        if axis == 2:
            return (zs.at[0, a], zr.at[0, a]), (zs.at[1, a], zr.at[1, a])
        return (face(axis, a, e), face(axis, a, 0)), (face(axis, a, 1), face(axis, a, e + 1))

    def halo_copies(axis, a):
        has_above, above, has_below, below = near[axis]
        up, down = ends(axis, a)
        made = []
        for k, (ends_k, mate) in enumerate(((up, above), (down, below))):
            made.append(pltpu.make_async_remote_copy(
                src_ref=ends_k[0], dst_ref=ends_k[1],
                send_sem=hsend.at[axis, a, k], recv_sem=hrecv.at[axis, a, k],
                device_id=mate, device_id_type=MESH,
            ))
        return made, (has_above, has_below)

    def halo_start(axis, a):
        made, has = halo_copies(axis, a)
        for k in range(2):

            @pl.when(has[k])
            def _(k=k):
                made[k].start()

    def halo_finish(axis, a):
        made, has = halo_copies(axis, a)
        for k in range(2):

            @pl.when(has[1 - k])
            def _(k=k):
                made[k].wait_recv()

            @pl.when(jnp.logical_not(has[1 - k]))
            def _(k=k):
                if axis == 0:
                    pad[a, 1, (0, e + 1)[k], pl.ds(1, e)] = jnp.zeros((e, e, ch), pad.dtype)
                elif axis == 1:
                    pad[a, 1, :, (0, e + 1)[k]] = jnp.zeros((e + 2, e, ch), pad.dtype)
                else:
                    zr[k, a] = jnp.zeros((e + 2, e + 2, ch), zr.dtype)

            @pl.when(has[k])
            def _(k=k):
                made[k].wait_send()

    halo_start(0, 0)
    halo_start(0, 1)

    zero = jnp.zeros((ch, ch), wx.dtype)

    def spread(t, carry):
        ox, oz = t // 3, lax.rem(t, 3)
        for i in range(4):
            for p in range(2):
                oy = i - p
                at = (pl.ds(i * ch, ch), pl.ds(p * ch, ch))
                if 0 <= oy <= 2:
                    wx[(0, t) + at] = w_ref[ox * 9 + oy * 3 + oz]
                    wx[(1, t) + at] = w_ref[(2 - ox) * 9 + (2 - oy) * 3 + 2 - oz].T
                else:
                    wx[(0, t) + at] = zero
                    wx[(1, t) + at] = zero
        return carry

    lax.fori_loop(0, 9, spread, 0)
    halo_finish(0, 0)
    halo_start(1, 0)

    def turn(c, carry):
        for x in range(2):
            own = pad[1, 1, 2 * c + x + 1, pl.ds(1, e)].reshape(half, 2, e, ch)
            for p in range(2):
                gt[c, pl.ds(p * ch, ch), pl.ds(x * half * e, half * e)] = (
                    own[:, p].reshape(half * e, ch).T
                )
        return carry

    lax.fori_loop(0, half, turn, 0)
    halo_finish(1, 0)

    def edges(a):
        def body(x, carry):
            v = pad[a, 1, x].astype(jnp.float32)
            zs[0, a, x] = v[:, e - 1]
            zs[1, a, x] = v[:, 0]
            return carry

        lax.fori_loop(0, e + 2, body, 0)

    edges(0)
    halo_start(2, 0)
    halo_finish(0, 1)
    halo_start(1, 1)
    halo_finish(2, 0)

    zidx = lax.broadcasted_iota(jnp.int32, (1, e, 1), 1)

    def shift(a):
        def body(x, carry):
            mid = pad[a, 1, x].astype(jnp.float32)
            lo = zr[0, a, x][:, None, :]
            hi = zr[1, a, x][:, None, :]
            pad[a, 0, x] = jnp.where(zidx == 0, lo, pltpu.roll(mid, 1, 1)).astype(pad.dtype)
            pad[a, 2, x] = jnp.where(zidx == e - 1, hi, pltpu.roll(mid, e - 1, 1)).astype(pad.dtype)
            return carry

        lax.fori_loop(0, e + 2, body, 0)

    def rows(a, oz, x0, nx):
        v = pad[a, oz, pl.ds(x0, nx)].reshape(nx, half + 1, 2, e, ch)
        parts = [
            v[:, i // 2:i // 2 + half, i % 2].reshape(nx * half * e, ch) for i in range(4)
        ]
        return jnp.concatenate(parts, axis=1)

    def terms(t, carry):
        ox, oz = t // 3, lax.rem(t, 3)
        acc = jnp.zeros((2 * ch, 4 * ch), jnp.float32)
        for c in range(half):
            acc = acc + jnp.dot(
                gt[c], rows(0, oz, ox + 2 * c, 2), preferred_element_type=jnp.float32
            )
        for oy in range(3):
            block = acc[:ch, oy * ch:(oy + 1) * ch] + acc[ch:, (oy + 1) * ch:(oy + 2) * ch]
            src[pl.ds(pl.multiple_of((t * 3 + oy) * ch, ch), ch)] = block.T
        return carry

    routes = []
    spot = 0
    for base, size, order in streams:
        off = base
        route = []
        for bit, mate in orders[order]:
            size = size // 2
            route.append((
                pl.multiple_of(off + bit * size, UNIT),
                pl.multiple_of(off + size - bit * size, UNIT),
                size, spot, mate,
            ))
            off = off + bit * size
            spot += size
        routes.append(route)
    flying = {}

    def begin(s, j):
        down = j < stages
        k = j if down else 2 * stages - 1 - j
        keep, give, size, at, mate = routes[s][k]
        if down:
            copy = pltpu.make_async_remote_copy(
                src_ref=src.at[pl.ds(give, size)], dst_ref=land.at[pl.ds(at, size)],
                send_sem=rsend.at[s, k], recv_sem=rrecv.at[s, k],
                device_id=mate, device_id_type=MESH,
            )
        else:
            copy = pltpu.make_async_remote_copy(
                src_ref=tot.at[pl.ds(keep, size)], dst_ref=tot.at[pl.ds(keep, size)],
                send_sem=gsend.at[s, k], recv_sem=grecv.at[s, k],
                device_id=mate, device_id_type=MESH,
            )
        copy.start()
        flying[s] = copy

    def end(s, j):
        flying[s].wait()
        if j < stages:
            keep, give, size, at, mate = routes[s][j]
            both = src[pl.ds(keep, size)] + land[pl.ds(at, size)]
            if j < stages - 1:
                src[pl.ds(keep, size)] = both
            else:
                tot[pl.ds(keep, size)] = both * factor

    nx = 4

    def conv(a, c):
        x0 = c * nx
        acc = jnp.zeros((nx * half * e, 2 * ch), jnp.float32)
        for t in range(9):
            acc = acc + jnp.dot(
                rows(a, t % 3, x0 + t // 3, nx), wx[a, t], preferred_element_type=jnp.float32
            )
        for p in range(2):
            obuf[a, pl.ds(x0, nx), :, p] = (
                acc[:, p * ch:(p + 1) * ch].reshape(nx, half, 2, BE, ch).astype(obuf.dtype)
            )

    def put(a, dst):
        for s in range(8):
            p = pos_ref[s]
            v = obuf[
                a, pl.ds(p // 4 * BE, BE), pl.ds(lax.rem(p // 2, 2) * (BE // 2), BE // 2), :,
                lax.rem(p, 2),
            ].reshape(BE, BE, BE, ch)
            dst[s] = jnp.where(s < cnt_ref[0], v, jnp.zeros_like(v))

    work = []
    for a, dst in ((0, out_ref), (1, dx_ref)):
        if a == 1:
            work.append(functools.partial(halo_finish, 2, 1))
            work.append(functools.partial(shift, 1))
        for c in range(e // nx):
            work.append(functools.partial(conv, a, c))
        work.append(functools.partial(put, a, dst))

    lead = streams[2][0]
    early = min(9, -(-lead // (3 * ch)))
    first = (0, 1)
    second = (2, 3)
    used = 3 * 9 * ch
    shift(0)
    if src.shape[0] > used:
        src[pl.ds(used, src.shape[0] - used)] = jnp.zeros((src.shape[0] - used, ch), src.dtype)
    lax.fori_loop(0, early, terms, 0)
    for s in first:
        begin(s, 0)
    halo_finish(1, 1)
    edges(1)
    halo_start(2, 1)
    if early < 9:
        lax.fori_loop(early, 9, terms, 0)
    last = 2 * stages - 1
    skew = 2
    for tau in range(1, last + 2 + skew):
        for group, j in ((first, tau), (second, tau - skew)):
            for s in group:
                if 1 <= j <= last + 1:
                    end(s, j - 1)
                if 0 <= j <= last:
                    begin(s, j)
        for _ in range(1 if tau < last + skew else len(work)):
            if work:
                work.pop(0)()

    def lay(t, carry):
        for oy in range(3):
            dw_ref[t // 3 * 9 + oy * 3 + lax.rem(t, 3)] = tot[
                pl.ds(pl.multiple_of((t * 3 + oy) * ch, ch), ch)
            ]
        return carry

    lax.fori_loop(0, 9, lay, 0)


def fused(features, cotangent, weight, pos, cnt, factor, n_tomo, n_brick):
    slots, vox, ch = features.shape
    e = 2 * BE
    half = e // 2
    n = n_tomo * n_brick
    tb, bb = n_tomo.bit_length() - 1, n_brick.bit_length() - 1
    stages = tb + bb
    rows = weight.shape[0] * ch
    unit = UNIT * n
    units = -(-rows // unit)
    units = max(units, 4)
    lead = 5 * 3 * ch // unit
    lead = min(lead, units // 2) if lead >= 2 else 2
    parts = [lead - lead // 2, lead // 2, units - lead - (units - lead) // 2, (units - lead) // 2]
    streams = []
    base = 0
    for k, u in enumerate(parts):
        streams.append((base, u * unit, k % 2))
        base += u * unit
    total = base
    vm = pl.BlockSpec(memory_space=pltpu.VMEM)
    sm = pl.BlockSpec(memory_space=pltpu.SMEM)
    brick = jax.ShapeDtypeStruct((slots, BE, BE, BE, ch), jnp.bfloat16)
    dma = pltpu.SemaphoreType.DMA
    return pl.pallas_call(
        functools.partial(kernel, factor, tb, bb, streams),
        out_shape=(brick, brick, jax.ShapeDtypeStruct(weight.shape, jnp.float32)),
        in_specs=[sm, sm, vm, vm, vm],
        out_specs=(vm, vm, vm),
        scratch_shapes=[
            pltpu.VMEM((2, 3, e + 2, e + 2, e, ch), jnp.bfloat16),
            pltpu.VMEM((2, 2, e + 2, e + 2, ch), jnp.float32),
            pltpu.VMEM((2, 2, e + 2, e + 2, ch), jnp.float32),
            pltpu.VMEM((2, 9, 4 * ch, 2 * ch), jnp.bfloat16),
            pltpu.VMEM((half, 2 * ch, 2 * half * e), jnp.bfloat16),
            pltpu.VMEM((2, e, half, 2, 2, BE, ch), jnp.bfloat16),
            pltpu.VMEM((total, ch), jnp.float32),
            pltpu.VMEM((total, ch), jnp.float32),
            pltpu.VMEM((total, ch), jnp.float32),
            dma((3, 2, 2)), dma((3, 2, 2)),
            dma((4, stages)), dma((4, stages)), dma((4, stages)), dma((4, stages)),
        ],
        compiler_params=pltpu.CompilerParams(
            collective_id=0, has_side_effects=True, vmem_limit_bytes=58 << 20
        ),
        name="fused",
    )(
        pos, cnt,
        features.reshape(slots, BE, BE, BE, ch), cotangent.reshape(slots, BE, BE, BE, ch), weight,
    )


def shards(features, weight, cotangent, brick_pos, brick_count):
    slots, vox, ch = features.shape[1:]
    n_tomo, n_brick = lax.axis_size("tomo"), lax.axis_size("brick")
    factor = 1.0 / math.sqrt(n_tomo * n_brick * slots * vox)
    out, dx, dw = fused(
        features[0], cotangent[0], weight, brick_pos[0], brick_count[0], factor, n_tomo, n_brick
    )
    return out.reshape(1, slots, vox, ch), dx.reshape(1, slots, vox, ch), dw


def solution(mesh):
    in_specs = (
        P("tomo", "brick", None, None),
        P(),
        P("tomo", "brick", None, None),
        P("tomo", "brick"),
        P("tomo", "brick"),
    )
    out_specs = (P("tomo", "brick", None, None), P("tomo", "brick", None, None), P())
    return jax.shard_map(shards, mesh=mesh, in_specs=in_specs, out_specs=out_specs, check_vma=False)
```
